32 devices in a mesh: point: 8 (over y, x, core), batch: 4 (over z).
Axes of the slice: x: 2, y: 2, z: 4, core: 2. Of those that a mesh axis runs over, the one named last changes fastest.
Arguments:
- activations: bfloat16 [128, 14, 14, 1024], P('batch'), may hold values from -8 to 8
- labels: int32 [128], P('batch'), may hold values from 0 to 999
- t_values: float32 [64], replicated, may hold values from 0 to 1
- point_index: int32 [8], replicated, may hold values from 0 to 63
- w_reduce: bfloat16 [3, 1024, 256], P(None, 'point'), may hold values from -1 to 1
- w_spatial: bfloat16 [3, 2304, 256], P(None, 'point'), may hold values from -0.125 to 0.125
- w_expand: bfloat16 [3, 256, 1024], P(None, 'point'), may hold values from -0.375 to 0.375
- w_classes: bfloat16 [3, 1000, 1024], P(None, None, 'point'), may hold values from -0.1875 to 0.1875
- norm_gain: float32 [3, 1536], replicated, may hold values from 0.5 to 1.5
- norm_bias: float32 [3, 1536], replicated, may hold values from -3 to 3
- class_bias: float32 [3, 1000], replicated, may hold values from -3 to 3
Outputs:
- mean_reduce: float32 [8, 256], P('point')
- var_reduce: float32 [8, 256], P('point')
- mean_spatial: float32 [8, 256], P('point')
- var_spatial: float32 [8, 256], P('point')
- mean_expand: float32 [8, 1024], P('point')
- var_expand: float32 [8, 1024], P('point')
- margin: float32 [8], replicated
The draws below stay inside these ranges and needn't reach their ends.
All inputs are finite; a program needn't handle non-finite values.
Results may differ from the reference program's by a relative error of at most 0.003.
Values may be sent and summed in bfloat16 or wider, within the bound.
A program may use at most 128 MiB of HBM per device.

```python
import jax
import jax.numpy as jnp
from jax import lax

CIN = 1024
MID = 256
CLASSES = 1000
SIDE = 14
TVALS = 64
NPOINTS = 8
IMGS = 128


def draw_activations(key, part):
    base_key, jitter_key = jax.random.split(key, 2)
    positions = jnp.arange(IMGS, dtype=jnp.float32) / max(IMGS - 1, 1)
    ramp_up = 3.0 ** positions
    jitter = jnp.exp(jax.random.uniform(jitter_key, (IMGS,), jnp.float32, -0.8, 0.8))
    values = jax.random.normal(base_key, (IMGS, SIDE, SIDE, CIN), jnp.float32)
    scales = (0.5 * ramp_up * jitter)[:, None, None, None]
    return jnp.clip(values * scales, -8.0, 8.0).astype(jnp.bfloat16)


def bend_ratio(key):
    return jax.random.uniform(jax.random.fold_in(key, 4242), (), jnp.float32, 0.9, 1.6)


def draw_w_reduce(key, part):
    ratio = bend_ratio(key)
    start_key, final_key = jax.random.split(jax.random.fold_in(key, 1717), 2)
    scale = CIN ** (-0.5)
    start = jnp.clip(jax.random.normal(start_key, (CIN, MID), jnp.float32), -3.0, 3.0) * scale
    final = jnp.clip(jax.random.normal(final_key, (CIN, MID), jnp.float32), -3.0, 3.0) * scale
    bend = -ratio * start
    return jnp.stack([start, bend, final], axis=0).astype(jnp.bfloat16)


def draw_t_values(key, part):
    ratio = bend_ratio(key)
    centre = 0.5 / (1.0 + ratio)
    drawn_key, near_key, pick_key = jax.random.split(jax.random.fold_in(key, 2929), 3)
    width = 0.0015
    drawn = jax.random.uniform(drawn_key, (TVALS,), jnp.float32, 0.0, 1.0)
    near = centre + jax.random.uniform(near_key, (TVALS,), jnp.float32, -width, width)
    picked = jax.random.permutation(pick_key, TVALS) < TVALS // 4
    return jnp.where(picked, near, drawn).astype(jnp.float32)


def set_ends(array, stream_key, low, largest):
    longest = array.shape.index(max(array.shape))
    spots = []
    for shift in (0, 1):
        where = [jax.random.randint(jax.random.fold_in(stream_key, axis), (), 0, length) for axis, length in enumerate(array.shape)]
        where[longest] = (where[longest] + shift) % array.shape[longest]
        spots.append(tuple(where))
    return array.at[spots[0]].set(low).at[spots[1]].set(largest)


def levels(rng, shape, cuts, low, top_value):
    gain = 1.0
    for position, shards_of in cuts:
        steps = jax.random.uniform(jax.random.fold_in(jax.random.fold_in(rng, 6), position), (shards_of,), jnp.float32, low / len(cuts), top_value / len(cuts))
        gain = gain * jnp.repeat(jnp.exp(steps), shape[position] // shards_of).reshape((-1,) + (1,) * (len(shape) - 1 - position))
    return gain


def noise(key, dims, scale, bound, shards=(), kind=jnp.bfloat16):
    result = jax.random.normal(key, dims, jnp.float32) * scale
    if len(shards) > 0:
        result = levels(key, dims, shards, -0.22, 0.18) * result
    return jnp.clip(result, min=-bound, max=bound).astype(kind)


def setup_inputs(seed: int = 0) -> dict:
    seeds = jax.random.split(jax.random.key(seed), 12)
    return {
        "activations": draw_activations(jax.random.fold_in(seeds[11], 71), 0),
        "labels": set_ends(jax.random.randint(seeds[1], (IMGS,), 0, CLASSES), jax.random.fold_in(seeds[1], 1), 0, CLASSES - 1).astype(jnp.int32),
        "t_values": draw_t_values(jax.random.fold_in(seeds[11], 71), 0),
        "point_index": set_ends(jax.random.randint(seeds[3], (NPOINTS,), 0, TVALS), jax.random.fold_in(seeds[3], 1), 0, TVALS - 1).astype(jnp.int32),
        "w_reduce": draw_w_reduce(jax.random.fold_in(seeds[11], 71), 0),
        "w_spatial": noise(seeds[5], (3, 9 * MID, MID), (9 * MID) ** -0.5, 0.125, ((1, 8),)),
        "w_expand": noise(seeds[6], (3, MID, CIN), MID ** -0.5, 0.375, ((1, 8),)),
        "w_classes": noise(seeds[7], (3, CLASSES, CIN), CIN ** -0.5, 0.1875, ((2, 8),)),
        "norm_gain": jnp.clip(jax.random.uniform(seeds[8], (3, 2 * MID + CIN), jnp.float32, 0.5, 1.5), 0.5, 1.5),
        "norm_bias": noise(seeds[9], (3, 2 * MID + CIN), 0.5, 3.0, (), jnp.float32),
        "class_bias": noise(seeds[10], (3, CLASSES), 0.5, 3.0, (), jnp.float32),
    }


EPSILON = 1e-05

def curve_coefficients(t_values, point_index):
    table_size = t_values.shape[0]
    matches = point_index[:, None] == jnp.arange(table_size, dtype=jnp.int32)[None, :]
    picked = lax.optimization_barrier(jnp.sum(jnp.where(matches, t_values[None, :], 0.0), axis=1))
    doubled = 2.0 * picked
    return jnp.stack([jnp.maximum(1.0 - doubled, 0.0), 1.0 - jnp.abs(1.0 - doubled), jnp.maximum(doubled - 1.0, 0.0)], axis=1)

def blend_all(coefficients, endpoints):
    target_shape = (coefficients.shape[0],) + (1,) * (endpoints.ndim - 1)
    start_part = coefficients[:, 0].reshape(target_shape) * endpoints[0].astype(jnp.float32)[None]
    bend_part = coefficients[:, 1].reshape(target_shape) * endpoints[1].astype(jnp.float32)[None]
    final_part = coefficients[:, 2].reshape(target_shape) * endpoints[2].astype(jnp.float32)[None]
    return start_part + bend_part + final_part

def normalize(pre_norm, gain_part, bias_part):
    channel_mean = lax.optimization_barrier(jnp.mean(pre_norm, axis=0))
    channel_var = lax.optimization_barrier(jnp.mean(jnp.square(pre_norm - channel_mean), axis=0))
    scaled = (pre_norm - channel_mean) * lax.rsqrt(channel_var + EPSILON) * gain_part + bias_part
    return (channel_mean, channel_var, scaled)

def spatial_conv(source, kernel):
    images, side_len, _, middle = source.shape
    padded = jnp.pad(source, ((0, 0), (1, 1), (1, 1), (0, 0)))
    summed = jnp.zeros((images * side_len * side_len, kernel.shape[1]), jnp.float32)
    for offset in range(9):
        shift_y, shift_x = (offset // 3, offset % 3)
        window = padded[:, shift_y:shift_y + side_len, shift_x:shift_x + side_len, :].reshape(images * side_len * side_len, middle)
        summed = summed + jnp.dot(window, kernel[offset * middle:(offset + 1) * middle], preferred_element_type=jnp.float32)
    return summed

def reference(activations, labels, t_values, point_index, w_reduce, w_spatial, w_expand, w_classes, norm_gain, norm_bias, class_bias):
    coefficients = curve_coefficients(t_values, point_index)
    flattened = activations.reshape(IMGS * SIDE * SIDE, CIN)
    onehot = labels[:, None] == jnp.arange(CLASSES, dtype=jnp.int32)[None, :]

    def one_point(coefficient_row):
        own_row = coefficient_row.reshape(1, 3)
        reduce_w = blend_all(own_row, w_reduce)[0].astype(jnp.bfloat16)
        spatial_w = blend_all(own_row, w_spatial)[0].astype(jnp.bfloat16)
        expand_w = blend_all(own_row, w_expand)[0].astype(jnp.bfloat16)
        class_w = blend_all(own_row, w_classes)[0].astype(jnp.bfloat16)
        gain_now = blend_all(own_row, norm_gain)[0]
        bias_now = blend_all(own_row, norm_bias)[0]
        shift_now = blend_all(own_row, class_bias)[0]
        reduced = jnp.dot(flattened, reduce_w, preferred_element_type=jnp.float32)
        mean_one, var_one, normed_one = normalize(reduced, gain_now[:MID], bias_now[:MID])
        first = jax.nn.relu(normed_one).astype(jnp.bfloat16).reshape(IMGS, SIDE, SIDE, MID)
        spatial = spatial_conv(first, spatial_w)
        mean_two, var_two, normed_two = normalize(spatial, gain_now[MID:2 * MID], bias_now[MID:2 * MID])
        second = jax.nn.relu(normed_two).astype(jnp.bfloat16)
        expanded = jnp.dot(second, expand_w, preferred_element_type=jnp.float32)
        mean_three, var_three, normed_three = normalize(expanded, gain_now[2 * MID:], bias_now[2 * MID:])
        block_out = jax.nn.relu(normed_three + flattened.astype(jnp.float32))
        pooled = lax.optimization_barrier(jnp.mean(block_out.reshape(IMGS, SIDE * SIDE, CIN), axis=1)).astype(jnp.bfloat16)
        logits = lax.dot_general(pooled, class_w, (((1,), (1,)), ((), ())), preferred_element_type=jnp.float32) + shift_now
        correct = lax.optimization_barrier(jnp.sum(jnp.where(onehot, logits, 0.0), axis=1))
        rivals = lax.optimization_barrier(jnp.max(jnp.where(onehot, -1e+30, logits), axis=1))
        margin_value = jnp.sum(correct - rivals) / IMGS
        return (mean_one, var_one, mean_two, var_two, mean_three, var_three, margin_value)
    results = lax.map(one_point, coefficients)
    return (results[0], results[1], results[2], results[3], results[4], results[5], results[6])
```

```python
import functools
import math

import jax
import jax.numpy as jnp
from jax import lax
from jax.experimental import pallas as pl
from jax.experimental.pallas import tpu as pltpu
from jax.sharding import PartitionSpec as P

EPSILON = 1e-05
MESH = pl.DeviceIdType.MESH
BF16 = jnp.bfloat16
F32 = jnp.float32


def round_up(value, step):
    return (value + step - 1) // step * step


def block_of(side):
    return 2 if side % 2 == 0 else 1


def dot(a, b, dims=((1,), (0,))):
    return lax.dot_general(a, b, (dims, ((), ())), preferred_element_type=F32)


def kernel(
    cfg,
    t_ref,
    index_ref,
    labels_ref,
    gain_ref,
    bias_ref,
    shift_ref,
    act_hbm,
    wr_hbm,
    ws_hbm,
    we_hbm,
    wc_hbm,
    mean1_out,
    var1_out,
    mean2_out,
    var2_out,
    mean3_out,
    var3_out,
    margin_out,
    act,
    anchor_r,
    anchor_s,
    anchor_e,
    anchor_c,
    send_r,
    send_s,
    send_e,
    send_c,
    recv_r,
    recv_s,
    recv_e,
    recv_c,
    rows_f32,
    wide,
    second,
    pooled_f32,
    pooled_all,
    stat1,
    stat2,
    stat3,
    label_all,
    score,
    margins,
    local_sem,
    act_sem,
    wsend,
    wrecv,
    zsend,
    zrecv,
    msend,
    mrecv,
):
    n, nb, images, side, cin, mid, classes, chunk, step = cfg
    blocks = side // step
    rows = step * side * images
    me = lax.axis_index("point")
    zz = lax.axis_index("batch")
    count = float(images * side * side * nb)
    start = jnp.minimum(zz * chunk, classes - chunk)
    start = pl.multiple_of(start, 8)

    barrier = pltpu.get_barrier_semaphore()
    for k in range(1, n):
        pl.semaphore_signal(
            barrier, inc=1, device_id=(lax.rem(me + k, n), zz), device_id_type=MESH
        )
    for k in range(1, nb):
        pl.semaphore_signal(
            barrier, inc=1, device_id=(me, lax.rem(zz + k, nb)), device_id_type=MESH
        )

    anchor_copies = []
    for i, (src, dst) in enumerate(
        (
            (wr_hbm, anchor_r),
            (ws_hbm, anchor_s),
            (we_hbm, anchor_e),
            (wc_hbm.at[:, pl.ds(start, chunk), :], anchor_c),
        )
    ):
        copy = pltpu.make_async_copy(src, dst, local_sem.at[i])
        copy.start()
        anchor_copies.append(copy)
    act_copies = []
    for b in range(blocks):
        copy = pltpu.make_async_copy(
            act_hbm.at[pl.ds(b * step, step)],
            act.at[pl.ds(b * step, step)],
            act_sem.at[b],
        )
        copy.start()
        act_copies.append(copy)

    def coefficients(point):
        doubled = 2.0 * t_ref[index_ref[point]]
        return (
            jnp.maximum(1.0 - doubled, 0.0),
            1.0 - jnp.abs(1.0 - doubled),
            jnp.maximum(doubled - 1.0, 0.0),
        )

    targets = [lax.rem(me + k, n) for k in range(n)]
    coefs = [coefficients(q) for q in targets]
    own = coefs[0]

    def blend(ends, c):
        return c[0] * ends[0] + c[1] * ends[1] + c[2] * ends[2]

    sends = []
    weights = (
        (anchor_r, send_r, recv_r),
        (anchor_s, send_s, recv_s),
        (anchor_e, send_e, recv_e),
        (anchor_c, send_c, recv_c),
    )
    for w, (anchor, send, recv) in enumerate(weights):
        anchor_copies[w].wait()
        total = anchor.shape[1]
        piece = 32 if total % 32 == 0 else 8

        def one(j, carry, anchor=anchor, send=send, recv=recv, piece=piece):
            at = pl.ds(pl.multiple_of(j * piece, piece), piece)
            ends = [anchor[a, at, :].astype(F32) for a in range(3)]
            for k in range(1, n):
                send[k - 1, at, :] = blend(ends, coefs[k]).astype(BF16)
            recv[me, at, :] = blend(ends, own).astype(BF16)
            return carry

        lax.fori_loop(0, total // piece, one, 0)
        if w == 0:
            pl.semaphore_wait(barrier, n - 1 + nb - 1)
        copies = []
        for k in range(1, n):
            copy = pltpu.make_async_remote_copy(
                src_ref=send.at[k - 1],
                dst_ref=recv.at[me],
                send_sem=wsend.at[w, k - 1],
                recv_sem=wrecv.at[w, k - 1],
                device_id=(targets[k], zz),
                device_id_type=MESH,
            )
            copy.start()
            copies.append(copy)
        sends.append(copies)

    def share(buffer, slot):
        copies = []
        for k in range(1, nb):
            copy = pltpu.make_async_remote_copy(
                src_ref=buffer.at[zz],
                dst_ref=buffer.at[zz],
                send_sem=zsend.at[slot, k - 1],
                recv_sem=zrecv.at[slot, k - 1],
                device_id=(me, lax.rem(zz + k, nb)),
                device_id_type=MESH,
            )
            copy.start()
            copies.append(copy)
        return copies

    label_all[zz] = labels_ref[...]
    label_copies = share(label_all, 5)

    for edge in (0, side + 1):
        wide[edge] = jnp.zeros(wide.shape[1:], BF16)
        wide[:, edge] = jnp.zeros((side + 2, images, mid), BF16)

    gain = blend([gain_ref[a : a + 1, :] for a in range(3)], own)
    bias = blend([bias_ref[a : a + 1, :] for a in range(3)], own)
    shift = blend([shift_ref[a : a + 1, :] for a in range(3)], own)

    def assemble(recv):
        value = recv[...]
        parts, depth, width = value.shape
        if depth % 16 == 0:
            return value.reshape(parts * depth, width)
        return value.astype(F32).reshape(parts * depth, width).astype(BF16)

    def finish(buffer):
        total = buffer[0]
        for z in range(1, nb):
            total = total + buffer[z]
        return total

    def scale_of(total, mean_out, var_out, low, high):
        mean = total[0:1] / count
        var = total[1:2] / count - mean * mean
        mean_out[...] = mean
        var_out[...] = var
        scale = lax.rsqrt(var + EPSILON) * gain[:, low:high]
        return scale, bias[:, low:high] - mean * scale

    for copy in sends[0]:
        copy.wait_recv()
    reduce_w = assemble(recv_r)
    for copy in act_copies:
        copy.wait()

    def reduce_step(b, carry):
        total, squares = carry
        x = act[pl.ds(b * step, step)].reshape(rows, cin)
        y = dot(x, reduce_w)
        rows_f32[b] = y
        return (
            total + jnp.sum(y, axis=0, keepdims=True),
            squares + jnp.sum(y * y, axis=0, keepdims=True),
        )

    zero = jnp.zeros((1, mid), F32)
    total, squares = lax.fori_loop(0, blocks, reduce_step, (zero, zero))
    stat1[zz, 0:1] = total
    stat1[zz, 1:2] = squares
    copies = share(stat1, 0)
    for copy in copies:
        copy.wait()
    scale1, offset1 = scale_of(finish(stat1), mean1_out, var1_out, 0, mid)

    def first_step(b, carry):
        y = jnp.maximum(rows_f32[b] * scale1 + offset1, 0.0)
        wide[pl.ds(b * step + 1, step), 1 : side + 1] = y.astype(BF16).reshape(
            step, side, images, mid
        )
        return carry

    lax.fori_loop(0, blocks, first_step, 0)

    for copy in sends[1]:
        copy.wait_recv()
    spatial_w = assemble(recv_s)

    def spatial_step(b, carry):
        total, squares = carry
        taps = [
            wide[pl.ds(b * step + dy, step), dx : dx + side].reshape(rows, mid)
            for dy in range(3)
            for dx in range(3)
        ]
        y = dot(jnp.concatenate(taps, axis=1), spatial_w)
        rows_f32[b] = y
        return (
            total + jnp.sum(y, axis=0, keepdims=True),
            squares + jnp.sum(y * y, axis=0, keepdims=True),
        )

    total, squares = lax.fori_loop(0, blocks, spatial_step, (zero, zero))
    stat2[zz, 0:1] = total
    stat2[zz, 1:2] = squares
    copies = share(stat2, 1)
    for copy in copies:
        copy.wait()
    scale2, offset2 = scale_of(finish(stat2), mean2_out, var2_out, mid, 2 * mid)

    def second_step(b, carry):
        gram, total = carry
        y = jnp.maximum(rows_f32[b] * scale2 + offset2, 0.0)
        y = y.astype(BF16)
        second[b] = y
        return (
            gram + dot(y, y, ((0,), (0,))),
            total + jnp.sum(y.astype(F32), axis=0, keepdims=True),
        )

    gram, total = lax.fori_loop(
        0, blocks, second_step, (jnp.zeros((mid, mid), F32), zero)
    )
    for copy in sends[2]:
        copy.wait_recv()
    expand_w = assemble(recv_e)

    def exact(a):
        high = a.astype(BF16)
        rest = a - high.astype(F32)
        middle = rest.astype(BF16)
        low = (rest - middle.astype(F32)).astype(BF16)
        return dot(high, expand_w) + (dot(middle, expand_w) + dot(low, expand_w))

    stat3[zz, 0:1] = exact(jnp.broadcast_to(total, (16, mid)))[0:1]
    stat3[zz, 1:2] = jnp.sum(exact(gram) * expand_w.astype(F32), axis=0, keepdims=True)
    copies = share(stat3, 2)
    for copy in copies:
        copy.wait()
    scale3, offset3 = scale_of(
        finish(stat3), mean3_out, var3_out, 2 * mid, 2 * mid + cin
    )

    area = side * images
    pooled_f32[...] = jnp.zeros_like(pooled_f32)

    def expand_step(i, carry):
        at = pl.ds(pl.multiple_of(lax.rem(i, step) * area, 16), area)
        x = second[i // step, at, :]
        wide_step = 256 if cin % 256 == 0 else cin
        for low in range(0, cin, wide_step):
            cut = slice(low, low + wide_step)
            e = dot(x, expand_w[:, cut]) * scale3[:, cut] + offset3[:, cut]
            e = e.reshape(side, images, wide_step) + act[i, :, :, cut].astype(F32)
            pooled_f32[:, cut] += jnp.sum(jnp.maximum(e, 0.0), axis=0)
        return carry

    lax.fori_loop(0, side, expand_step, 0)
    pooled_all[zz] = (pooled_f32[...] / float(side * side)).astype(BF16)
    copies = share(pooled_all, 3)
    for copy in sends[3]:
        copy.wait_recv()
    for copy in copies:
        copy.wait()
    for copy in label_copies:
        copy.wait()

    pooled = pooled_all[...].reshape(nb * images, cin)
    width = cin // n
    logits = None
    for q in range(n):
        term = dot(recv_c[q], pooled[:, q * width : (q + 1) * width], ((1,), (1,)))
        logits = term if logits is None else logits + term
    all_ids = lax.broadcasted_iota(jnp.int32, (chunk, classes), 1)
    own_ids = lax.broadcasted_iota(jnp.int32, (chunk, classes), 0) + start
    shift_column = jnp.sum(
        jnp.where(all_ids == own_ids, jnp.broadcast_to(shift, (chunk, classes)), 0.0),
        axis=1,
        keepdims=True,
    )
    logits = logits + shift_column
    class_ids = lax.broadcasted_iota(jnp.int32, (chunk, 1), 0) + start
    fresh = class_ids >= zz * chunk
    for z in range(nb):
        part = logits[:, z * images : (z + 1) * images]
        hit = class_ids == label_all[z]
        score[zz, z, 0:1] = jnp.sum(
            jnp.where(jnp.logical_and(hit, fresh), part, 0.0), axis=0, keepdims=True
        )
        score[zz, z, 1:2] = jnp.max(jnp.where(hit, -1e30, part), axis=0, keepdims=True)
    copies = share(score, 4)
    for copy in copies:
        copy.wait()
    correct = score[0, :, 0:1]
    rival = score[0, :, 1:2]
    for z in range(1, nb):
        correct = correct + score[z, :, 0:1]
        rival = jnp.maximum(rival, score[z, :, 1:2])
    margin = jnp.sum(jnp.sum(correct - rival, axis=2, keepdims=True), axis=0) / float(
        nb * images
    )
    margins[me] = jnp.broadcast_to(margin, margins.shape[1:])
    copies = []
    for k in range(1, n):
        copy = pltpu.make_async_remote_copy(
            src_ref=margins.at[me],
            dst_ref=margins.at[me],
            send_sem=msend.at[k - 1],
            recv_sem=mrecv.at[k - 1],
            device_id=(targets[k], zz),
            device_id_type=MESH,
        )
        copy.start()
        copies.append(copy)
    for group in sends:
        for copy in group:
            copy.wait_send()
    for copy in copies:
        copy.wait()
    lanes = lax.broadcasted_iota(jnp.int32, (1, 128), 1)
    result = jnp.zeros((1, 128), F32)
    for q in range(n):
        result = jnp.where(lanes == q, margins[q, 0:1, :], result)
    margin_out[...] = result


def shards(
    n,
    nb,
    activations,
    labels,
    t_values,
    point_index,
    w_reduce,
    w_spatial,
    w_expand,
    w_classes,
    norm_gain,
    norm_bias,
    class_bias,
):
    images, side, _, cin = activations.shape
    mid = w_reduce.shape[2]
    classes = w_classes.shape[1]
    chunk = round_up(-(-classes // nb), 16)
    step = block_of(side)
    blocks = side // step
    rows = step * side * images
    cfg = (n, nb, images, side, cin, mid, classes, chunk, step)
    smem = pl.BlockSpec(memory_space=pltpu.SMEM)
    vmem = pl.BlockSpec(memory_space=pltpu.VMEM)
    hbm = pl.BlockSpec(memory_space=pltpu.HBM)

    def slices(parts):
        return [
            pltpu.VMEM((parts,) + w_reduce.shape[1:], BF16),
            pltpu.VMEM((parts,) + w_spatial.shape[1:], BF16),
            pltpu.VMEM((parts,) + w_expand.shape[1:], BF16),
            pltpu.VMEM((parts, chunk, w_classes.shape[2]), BF16),
        ]

    dma = pltpu.SemaphoreType.DMA
    outs = pl.pallas_call(
        functools.partial(kernel, cfg),
        out_shape=[
            jax.ShapeDtypeStruct((1, mid), F32),
            jax.ShapeDtypeStruct((1, mid), F32),
            jax.ShapeDtypeStruct((1, mid), F32),
            jax.ShapeDtypeStruct((1, mid), F32),
            jax.ShapeDtypeStruct((1, cin), F32),
            jax.ShapeDtypeStruct((1, cin), F32),
            jax.ShapeDtypeStruct((1, 128), F32),
        ],
        in_specs=[smem, smem, vmem, vmem, vmem, vmem, hbm, hbm, hbm, hbm, hbm],
        out_specs=[vmem] * 7,
        scratch_shapes=[
            pltpu.VMEM((side, side, images, cin), BF16),
            *slices(3),
            *slices(n - 1),
            *slices(n),
            pltpu.VMEM((blocks, rows, mid), F32),
            pltpu.VMEM((side + 2, side + 2, images, mid), BF16),
            pltpu.VMEM((blocks, rows, mid), BF16),
            pltpu.VMEM((images, cin), F32),
            pltpu.VMEM((nb, images, cin), BF16),
            pltpu.VMEM((nb, 2, mid), F32),
            pltpu.VMEM((nb, 2, mid), F32),
            pltpu.VMEM((nb, 2, cin), F32),
            pltpu.VMEM((nb, 1, images), jnp.int32),
            pltpu.VMEM((nb, nb, 2, images), F32),
            pltpu.VMEM((n, 8, 128), F32),
            dma((4,)),
            dma((blocks,)),
            dma((4, n - 1)),
            dma((4, n - 1)),
            dma((6, nb - 1)),
            dma((6, nb - 1)),
            dma((n - 1,)),
            dma((n - 1,)),
        ],
        compiler_params=pltpu.CompilerParams(
            collective_id=0, has_side_effects=True, vmem_limit_bytes=62 * 1024 * 1024
        ),
    )(
        t_values,
        point_index,
        labels[None, :],
        norm_gain,
        norm_bias,
        class_bias,
        jnp.transpose(activations, (1, 2, 0, 3)),
        w_reduce,
        w_spatial,
        w_expand,
        w_classes,
    )
    return (*outs[:6], outs[6][0, : point_index.shape[0]])


def solution(mesh):
    n, nb = mesh.shape["point"], mesh.shape["batch"]
    placed = (
        P("batch", None, None, None),
        P("batch"),
        P(),
        P(),
        P(None, "point", None),
        P(None, "point", None),
        P(None, "point", None),
        P(None, None, "point"),
        P(),
        P(),
        P(),
    )
    return jax.shard_map(
        functools.partial(shards, n, nb),
        mesh=mesh,
        in_specs=placed,
        out_specs=(
            P("point", None),
            P("point", None),
            P("point", None),
            P("point", None),
            P("point", None),
            P("point", None),
            P(),
        ),
        check_vma=False,
    )
```

```python
import functools

import jax
import jax.numpy as jnp
from jax import lax
from jax.experimental import pallas as pl
from jax.experimental.pallas import tpu as pltpu
from jax.sharding import PartitionSpec as P

EPSILON = 1e-05
MESH = pl.DeviceIdType.MESH
BF16 = jnp.bfloat16
F32 = jnp.float32


def block_of(side):
    return 2 if side % 2 == 0 else 1


def dot(a, b, dims=((1,), (0,))):
    return lax.dot_general(a, b, (dims, ((), ())), preferred_element_type=F32)


def kernel(
    cfg,
    t_ref,
    index_ref,
    labels_ref,
    gain_ref,
    bias_ref,
    shift_ref,
    act_hbm,
    wr_hbm,
    ws_hbm,
    we_hbm,
    wc_hbm,
    mean1_out,
    var1_out,
    mean2_out,
    var2_out,
    mean3_out,
    var3_out,
    margin_out,
    act,
    anchor_r,
    anchor_s,
    anchor_e,
    anchor_c,
    send_r,
    send_s,
    send_e,
    send_c,
    recv_r,
    recv_s,
    recv_e,
    recv_c,
    rows_f32,
    wide,
    second,
    pooled_f32,
    shift_col,
    stat1,
    stat2,
    stat3,
    margins,
    local_sem,
    act_sem,
    wsend,
    wrecv,
    zsend,
    zrecv,
    msend,
    mrecv,
):
    n, nb, images, side, cin, mid, classes, step = cfg
    blocks = side // step
    rows = step * side * images
    me = lax.axis_index("point")
    zz = lax.axis_index("batch")
    count = float(images * side * side * nb)
    others = [
        (lax.rem(me + k, n), lax.rem(zz + j, nb))
        for k in range(n)
        for j in range(nb)
        if k or j
    ]

    barrier = pltpu.get_barrier_semaphore()
    for other in others:
        pl.semaphore_signal(barrier, inc=1, device_id=other, device_id_type=MESH)

    anchor_copies = []
    for i, (src, dst) in enumerate(
        (
            (wr_hbm, anchor_r),
            (ws_hbm, anchor_s),
            (we_hbm, anchor_e),
            (wc_hbm, anchor_c),
        )
    ):
        copy = pltpu.make_async_copy(src, dst, local_sem.at[i])
        copy.start()
        anchor_copies.append(copy)
    act_copies = []
    for b in range(blocks):
        copy = pltpu.make_async_copy(
            act_hbm.at[pl.ds(b * step, step)],
            act.at[pl.ds(b * step, step)],
            act_sem.at[b],
        )
        copy.start()
        act_copies.append(copy)

    def coefficients(point):
        doubled = 2.0 * t_ref[index_ref[point]]
        return (
            jnp.maximum(1.0 - doubled, 0.0),
            1.0 - jnp.abs(1.0 - doubled),
            jnp.maximum(doubled - 1.0, 0.0),
        )

    targets = [lax.rem(me + k, n) for k in range(n)]
    coefs = [coefficients(q) for q in targets]
    own = coefs[0]

    def blend(ends, c):
        return c[0] * ends[0] + c[1] * ends[1] + c[2] * ends[2]

    sends = []
    weights = (
        (anchor_r, send_r, recv_r),
        (anchor_s, send_s, recv_s),
        (anchor_e, send_e, recv_e),
        (anchor_c, send_c, recv_c),
    )

    def blend_and_send(w):
        anchor, send, recv = weights[w]
        anchor_copies[w].wait()
        total = anchor.shape[1]
        piece = 64 if anchor.shape[2] <= 128 else 32

        def part(at):
            ends = [anchor[a, at, :].astype(F32) for a in range(3)]
            for k in range(1, n):
                send[k - 1, at, :] = blend(ends, coefs[k]).astype(BF16)
            recv[me, at, :] = blend(ends, own).astype(BF16)

        def one(j, carry):
            part(pl.ds(pl.multiple_of(j * piece, piece), piece))
            return carry

        lax.fori_loop(0, total // piece, one, 0)
        if total % piece:
            part(pl.ds(total - total % piece, total % piece))
        if w == 0:
            pl.semaphore_wait(barrier, n * nb - 1)
        copies = []
        for k in range(1, n):
            copy = pltpu.make_async_remote_copy(
                src_ref=send.at[k - 1],
                dst_ref=recv.at[me],
                send_sem=wsend.at[w, k - 1],
                recv_sem=wrecv.at[w, k - 1],
                device_id=(targets[k], zz),
                device_id_type=MESH,
            )
            copy.start()
            copies.append(copy)
        sends.append(copies)

    for w in range(3):
        blend_and_send(w)

    def share(buffer, slot):
        copies = []
        for k in range(1, nb):
            copy = pltpu.make_async_remote_copy(
                src_ref=buffer.at[zz],
                dst_ref=buffer.at[zz],
                send_sem=zsend.at[slot, k - 1],
                recv_sem=zrecv.at[slot, k - 1],
                device_id=(me, lax.rem(zz + k, nb)),
                device_id_type=MESH,
            )
            copy.start()
            copies.append(copy)
        return copies

    for edge in (0, side + 1):
        wide[edge] = jnp.zeros(wide.shape[1:], BF16)
        wide[:, edge] = jnp.zeros((side + 2, images, mid), BF16)

    gain = blend([gain_ref[a : a + 1, :] for a in range(3)], own)
    bias = blend([bias_ref[a : a + 1, :] for a in range(3)], own)
    shift = blend([shift_ref[a : a + 1, :] for a in range(3)], own)

    def assemble(recv):
        value = recv[...]
        parts, depth, width = value.shape
        if depth % 16 == 0:
            return value.reshape(parts * depth, width)
        return value.astype(F32).reshape(parts * depth, width).astype(BF16)

    def finish(buffer):
        total = buffer[0]
        for z in range(1, nb):
            total = total + buffer[z]
        return total

    def scale_of(total, mean_out, var_out, low, high):
        mean = total[0:1] / count
        var = total[1:2] / count - mean * mean
        mean_out[...] = mean
        var_out[...] = var
        scale = lax.rsqrt(var + EPSILON) * gain[:, low:high]
        return scale, bias[:, low:high] - mean * scale

    piece = 128
    for low in range(0, classes, piece):
        high = min(classes, low + piece)
        size = high - low
        square = lax.broadcasted_iota(jnp.int32, (size, size), 0) == (
            lax.broadcasted_iota(jnp.int32, (size, size), 1)
        )
        shift_col[low:high, :] = jnp.sum(
            jnp.where(square, shift[:, low:high], 0.0), axis=1, keepdims=True
        )

    for copy in sends[0]:
        copy.wait_recv()
    reduce_w = assemble(recv_r)
    for copy in act_copies:
        copy.wait()

    def reduce_step(b, carry):
        total, squares = carry
        x = act[pl.ds(b * step, step)].reshape(rows, cin)
        y = dot(x, reduce_w)
        rows_f32[b] = y
        return (
            total + jnp.sum(y, axis=0, keepdims=True),
            squares + jnp.sum(y * y, axis=0, keepdims=True),
        )

    zero = jnp.zeros((1, mid), F32)
    total, squares = lax.fori_loop(0, blocks, reduce_step, (zero, zero))
    stat1[zz, 0:1] = total
    stat1[zz, 1:2] = squares
    copies = share(stat1, 0)
    blend_and_send(3)
    for copy in copies:
        copy.wait()
    scale1, offset1 = scale_of(finish(stat1), mean1_out, var1_out, 0, mid)

    def first_step(b, carry):
        y = jnp.maximum(rows_f32[b] * scale1 + offset1, 0.0)
        wide[pl.ds(b * step + 1, step), 1 : side + 1] = y.astype(BF16).reshape(
            step, side, images, mid
        )
        return carry

    lax.fori_loop(0, blocks, first_step, 0)

    for copy in sends[1]:
        copy.wait_recv()
    spatial_w = assemble(recv_s)

    def spatial_step(b, carry):
        total, squares = carry
        taps = [
            wide[pl.ds(b * step + dy, step), dx : dx + side].reshape(rows, mid)
            for dy in range(3)
            for dx in range(3)
        ]
        y = dot(jnp.concatenate(taps, axis=1), spatial_w)
        rows_f32[b] = y
        return (
            total + jnp.sum(y, axis=0, keepdims=True),
            squares + jnp.sum(y * y, axis=0, keepdims=True),
        )

    total, squares = lax.fori_loop(0, blocks, spatial_step, (zero, zero))
    stat2[zz, 0:1] = total
    stat2[zz, 1:2] = squares
    copies = share(stat2, 1)
    for copy in copies:
        copy.wait()
    scale2, offset2 = scale_of(finish(stat2), mean2_out, var2_out, mid, 2 * mid)

    def second_step(b, carry):
        gram, total = carry
        y = jnp.maximum(rows_f32[b] * scale2 + offset2, 0.0)
        y = y.astype(BF16)
        second[b] = y
        return (
            gram + dot(y, y, ((0,), (0,))),
            total + jnp.sum(y.astype(F32), axis=0, keepdims=True),
        )

    gram, total = lax.fori_loop(
        0, blocks, second_step, (jnp.zeros((mid, mid), F32), zero)
    )
    for copy in sends[2]:
        copy.wait_recv()
    expand_w = assemble(recv_e)

    def exact(a):
        high = a.astype(BF16)
        rest = a - high.astype(F32)
        middle = rest.astype(BF16)
        low = (rest - middle.astype(F32)).astype(BF16)
        return dot(high, expand_w) + (dot(middle, expand_w) + dot(low, expand_w))

    stat3[zz, 0:1] = exact(jnp.broadcast_to(total, (16, mid)))[0:1]
    stat3[zz, 1:2] = jnp.sum(exact(gram) * expand_w.astype(F32), axis=0, keepdims=True)
    copies = share(stat3, 2)
    for copy in copies:
        copy.wait()
    scale3, offset3 = scale_of(
        finish(stat3), mean3_out, var3_out, 2 * mid, 2 * mid + cin
    )

    area = side * images
    pooled_f32[...] = jnp.zeros_like(pooled_f32)

    def expand_step(i, carry):
        at = pl.ds(pl.multiple_of(lax.rem(i, step) * area, 16), area)
        x = second[i // step, at, :]
        wide_step = 256 if cin % 256 == 0 else cin
        for low in range(0, cin, wide_step):
            cut = slice(low, low + wide_step)
            e = dot(x, expand_w[:, cut]) * scale3[:, cut] + offset3[:, cut]
            e = e.reshape(side, images, wide_step) + act[i, :, :, cut].astype(F32)
            pooled_f32[:, cut] += jnp.sum(jnp.maximum(e, 0.0), axis=0)
        return carry

    lax.fori_loop(0, side, expand_step, 0)
    pooled = (pooled_f32[...] / float(side * side)).astype(BF16)
    for copy in sends[3]:
        copy.wait_recv()

    width = cin // n
    if width % 128 == 0:
        class_w = jnp.concatenate([recv_c[q] for q in range(n)], axis=1)
        logits = dot(class_w, pooled, ((1,), (1,)))
    else:
        logits = jnp.zeros((classes, images), F32)
        for q in range(n):
            part = pooled[:, q * width : (q + 1) * width]
            logits = logits + dot(recv_c[q], part, ((1,), (1,)))
    logits = logits + shift_col[...]
    class_ids = lax.broadcasted_iota(jnp.int32, (classes, images), 0)
    hit = class_ids == labels_ref[...]
    correct = jnp.sum(jnp.where(hit, logits, 0.0), axis=0, keepdims=True)
    rival = jnp.max(jnp.where(hit, -1e30, logits), axis=0, keepdims=True)
    margin = jnp.sum(correct - rival, axis=1, keepdims=True) / float(nb * images)
    mine = me * nb + zz
    margins[mine] = jnp.broadcast_to(margin, margins.shape[1:])
    copies = []
    for i, other in enumerate(others):
        copy = pltpu.make_async_remote_copy(
            src_ref=margins.at[mine],
            dst_ref=margins.at[mine],
            send_sem=msend.at[i],
            recv_sem=mrecv.at[i],
            device_id=other,
            device_id_type=MESH,
        )
        copy.start()
        copies.append(copy)
    for group in sends:
        for copy in group:
            copy.wait_send()
    for copy in copies:
        copy.wait()
    lanes = lax.broadcasted_iota(jnp.int32, (1, 128), 1)
    result = jnp.zeros((1, 128), F32)
    for q in range(n):
        part = margins[q * nb]
        for z in range(1, nb):
            part = part + margins[q * nb + z]
        result = jnp.where(lanes == q, part, result)
    margin_out[...] = result


def hand_over(*refs):
    for source, target in zip(refs[:6], refs[7:13]):
        target[...] = source[...]
    points = refs[13].shape[0]
    refs[13][...] = refs[6][0, 0:points]


def shards(
    n,
    nb,
    activations,
    labels,
    t_values,
    point_index,
    w_reduce,
    w_spatial,
    w_expand,
    w_classes,
    norm_gain,
    norm_bias,
    class_bias,
):
    images, side, _, cin = activations.shape
    mid = w_reduce.shape[2]
    classes = w_classes.shape[1]
    step = block_of(side)
    blocks = side // step
    rows = step * side * images
    cfg = (n, nb, images, side, cin, mid, classes, step)
    smem = pl.BlockSpec(memory_space=pltpu.SMEM)
    vmem = pl.BlockSpec(memory_space=pltpu.VMEM)
    hbm = pl.BlockSpec(memory_space=pltpu.HBM)

    def slices(parts):
        return [
            pltpu.VMEM((parts,) + w_reduce.shape[1:], BF16),
            pltpu.VMEM((parts,) + w_spatial.shape[1:], BF16),
            pltpu.VMEM((parts,) + w_expand.shape[1:], BF16),
            pltpu.VMEM((parts,) + w_classes.shape[1:], BF16),
        ]

    dma = pltpu.SemaphoreType.DMA
    outs = pl.pallas_call(
        functools.partial(kernel, cfg),
        out_shape=[
            jax.ShapeDtypeStruct((1, mid), F32),
            jax.ShapeDtypeStruct((1, mid), F32),
            jax.ShapeDtypeStruct((1, mid), F32),
            jax.ShapeDtypeStruct((1, mid), F32),
            jax.ShapeDtypeStruct((1, cin), F32),
            jax.ShapeDtypeStruct((1, cin), F32),
            jax.ShapeDtypeStruct((1, 128), F32),
        ],
        in_specs=[smem, smem, vmem, vmem, vmem, vmem, hbm, hbm, hbm, hbm, hbm],
        out_specs=[vmem] * 7,
        scratch_shapes=[
            pltpu.VMEM((side, side, images, cin), BF16),
            *slices(3),
            *slices(n - 1),
            *slices(n),
            pltpu.VMEM((blocks, rows, mid), F32),
            pltpu.VMEM((side + 2, side + 2, images, mid), BF16),
            pltpu.VMEM((blocks, rows, mid), BF16),
            pltpu.VMEM((images, cin), F32),
            pltpu.VMEM((classes, 1), F32),
            pltpu.VMEM((nb, 2, mid), F32),
            pltpu.VMEM((nb, 2, mid), F32),
            pltpu.VMEM((nb, 2, cin), F32),
            pltpu.VMEM((n * nb, 1, 128), F32),
            dma((4,)),
            dma((blocks,)),
            dma((4, n - 1)),
            dma((4, n - 1)),
            dma((3, nb - 1)),
            dma((3, nb - 1)),
            dma((n * nb - 1,)),
            dma((n * nb - 1,)),
        ],
        compiler_params=pltpu.CompilerParams(
            collective_id=0, has_side_effects=True, vmem_limit_bytes=62 * 1024 * 1024
        ),
    )(
        t_values,
        point_index,
        labels[None, :],
        norm_gain,
        norm_bias,
        class_bias,
        jnp.transpose(activations, (1, 2, 0, 3)),
        w_reduce,
        w_spatial,
        w_expand,
        w_classes,
    )
    points = point_index.shape[0]
    return pl.pallas_call(
        hand_over,
        out_shape=[jax.ShapeDtypeStruct(o.shape, F32) for o in outs[:6]]
        + [jax.ShapeDtypeStruct((points,), F32)],
        in_specs=[vmem] * 7,
        out_specs=[vmem] * 7,
    )(*outs)


def solution(mesh):
    n, nb = mesh.shape["point"], mesh.shape["batch"]
    placed = (
        P("batch", None, None, None),
        P("batch"),
        P(),
        P(),
        P(None, "point", None),
        P(None, "point", None),
        P(None, "point", None),
        P(None, None, "point"),
        P(),
        P(),
        P(),
    )
    return jax.shard_map(
        functools.partial(shards, n, nb),
        mesh=mesh,
        in_specs=placed,
        out_specs=(
            P("point", None),
            P("point", None),
            P("point", None),
            P("point", None),
            P("point", None),
            P("point", None),
            P(),
        ),
        check_vma=False,
    )
```

```python
import functools

import jax
import jax.numpy as jnp
from jax import lax
from jax.experimental import pallas as pl
from jax.experimental.pallas import tpu as pltpu
from jax.sharding import PartitionSpec as P

EPSILON = 1e-05
MESH = pl.DeviceIdType.MESH
BF16 = jnp.bfloat16
F32 = jnp.float32


def block_of(side):
    return 2 if side % 2 == 0 else 1


def dot(a, b, dims=((1,), (0,))):
    return lax.dot_general(a, b, (dims, ((), ())), preferred_element_type=F32)


def kernel(
    cfg,
    t_ref,
    index_ref,
    labels_ref,
    gain_ref,
    bias_ref,
    shift_ref,
    act_hbm,
    wr_hbm,
    ws_hbm,
    we_hbm,
    wc_hbm,
    mean1_out,
    var1_out,
    mean2_out,
    var2_out,
    mean3_out,
    var3_out,
    margin_out,
    act,
    anchor_r,
    anchor_s,
    anchor_e,
    anchor_c,
    send_r,
    send_s,
    send_e,
    send_c,
    recv_r,
    recv_s,
    recv_e,
    recv_c,
    rows_f32,
    wide,
    second,
    pooled_f32,
    shift_col,
    stat1,
    stat2,
    stat3,
    margins,
    local_sem,
    act_sem,
    wsend,
    wrecv,
    pair,
    zsend,
    zrecv,
    msend,
    mrecv,
):
    n, nb, images, side, cin, mid, classes, step = cfg
    blocks = side // step
    rows = step * side * images
    me = lax.axis_index("point")
    zz = lax.axis_index("batch")
    count = float(images * side * side * nb)
    others = [
        (lax.rem(me + k, n), lax.rem(zz + j, nb))
        for k in range(n)
        for j in range(nb)
        if k or j
    ]

    barrier = pltpu.get_barrier_semaphore()
    for other in others:
        pl.semaphore_signal(barrier, inc=1, device_id=other, device_id_type=MESH)

    anchor_copies = []
    for i, (src, dst) in enumerate(
        (
            (wr_hbm, anchor_r),
            (ws_hbm, anchor_s),
            (we_hbm, anchor_e),
            (wc_hbm, anchor_c),
        )
    ):
        copy = pltpu.make_async_copy(src, dst, local_sem.at[i])
        copy.start()
        anchor_copies.append(copy)
    act_copies = []
    for b in range(blocks):
        copy = pltpu.make_async_copy(
            act_hbm.at[pl.ds(b * step, step)],
            act.at[pl.ds(b * step, step)],
            act_sem.at[b],
        )
        copy.start()
        act_copies.append(copy)

    def coefficients(point):
        doubled = 2.0 * t_ref[index_ref[point]]
        return (
            jnp.maximum(1.0 - doubled, 0.0),
            1.0 - jnp.abs(1.0 - doubled),
            jnp.maximum(doubled - 1.0, 0.0),
        )

    targets = [lax.rem(me + k, n) for k in range(n)]
    coefs = [coefficients(q) for q in targets]
    own = coefs[0]

    def blend(ends, c):
        return c[0] * ends[0] + c[1] * ends[1] + c[2] * ends[2]

    sends = []
    weights = (
        (anchor_r, send_r, recv_r),
        (anchor_s, send_s, recv_s),
        (anchor_e, send_e, recv_e),
        (anchor_c, send_c, recv_c),
    )

    half = classes // 4 // 64 * 64 + 64 if nb % 2 == 0 else 0
    low_bit = lax.rem(zz, 2)
    mine_low = pl.multiple_of(low_bit * half, 8)
    rest_rows = pl.ds(2 * half, classes - 2 * half)

    def whole(w):
        return pl.ds(0, weights[w][0].shape[1])

    def blend_and_send(w):
        anchor, send, recv = weights[w]
        anchor_copies[w].wait()
        total = anchor.shape[1]
        piece = 64 if anchor.shape[2] <= 128 else 32

        def part(at):
            ends = [anchor[a, at, :].astype(F32) for a in range(3)]
            for k in range(1, n):
                send[k - 1, at, :] = blend(ends, coefs[k]).astype(BF16)
            recv[me, at, :] = blend(ends, own).astype(BF16)

        pieces = []
        if w < 3:
            spans = ((0, total),)
            pieces.append((w, whole(w)))
        else:
            spans = ((mine_low, half), (2 * half, total - 2 * half))
            if half:
                pieces.append((3, pl.ds(mine_low, half)))
            pieces.append((4, rest_rows))
        for low, size in spans:

            def one(j, carry):
                part(pl.ds(pl.multiple_of(low + j * piece, 8), piece))
                return carry

            lax.fori_loop(0, size // piece, one, 0)
            if size % piece:
                part(pl.ds(low + size - size % piece, size % piece))
        if w == 0:
            pl.semaphore_wait(barrier, n * nb - 1)
        for slot, at in pieces:
            copies = []
            for k in range(n - 1, 0, -1):
                copy = pltpu.make_async_remote_copy(
                    src_ref=send.at[k - 1, at],
                    dst_ref=recv.at[me, at],
                    send_sem=wsend.at[slot, k],
                    recv_sem=wrecv.at[slot, me],
                    device_id=(targets[k], zz),
                    device_id_type=MESH,
                )
                copy.start()
                copies.append(copy)
            sends.append(copies)

    def arrived(slot, sender, at):
        recv = weights[min(slot, 3)][2]
        pltpu.make_async_remote_copy(
            src_ref=recv.at[sender, at],
            dst_ref=recv.at[sender, at],
            send_sem=wsend.at[slot, 0],
            recv_sem=wrecv.at[slot, sender],
            device_id=(targets[1], zz),
            device_id_type=MESH,
        ).wait_recv()

    def all_arrived(slot, at):
        for k in range(1, n):
            arrived(slot, targets[k], at)

    for w in range(3):
        blend_and_send(w)

    def share(buffer, slot):
        copies = []
        for k in range(1, nb):
            copy = pltpu.make_async_remote_copy(
                src_ref=buffer.at[zz],
                dst_ref=buffer.at[zz],
                send_sem=zsend.at[slot, k - 1],
                recv_sem=zrecv.at[slot, k - 1],
                device_id=(me, lax.rem(zz + k, nb)),
                device_id_type=MESH,
            )
            copy.start()
            copies.append(copy)
        return copies

    for edge in (0, side + 1):
        wide[edge] = jnp.zeros(wide.shape[1:], BF16)
        wide[:, edge] = jnp.zeros((side + 2, images, mid), BF16)

    gain = blend([gain_ref[a : a + 1, :] for a in range(3)], own)
    bias = blend([bias_ref[a : a + 1, :] for a in range(3)], own)
    shift = blend([shift_ref[a : a + 1, :] for a in range(3)], own)

    def assemble(recv):
        value = recv[...]
        parts, depth, width = value.shape
        if depth % 16 == 0:
            return value.reshape(parts * depth, width)
        return value.astype(F32).reshape(parts * depth, width).astype(BF16)

    def finish(buffer):
        total = buffer[0]
        for z in range(1, nb):
            total = total + buffer[z]
        return total

    def scale_of(total, mean_out, var_out, low, high):
        mean = total[0:1] / count
        var = total[1:2] / count - mean * mean
        mean_out[...] = mean
        var_out[...] = var
        scale = lax.rsqrt(var + EPSILON) * gain[:, low:high]
        return scale, bias[:, low:high] - mean * scale

    piece = 128
    for low in range(0, classes, piece):
        high = min(classes, low + piece)
        size = high - low
        square = lax.broadcasted_iota(jnp.int32, (size, size), 0) == (
            lax.broadcasted_iota(jnp.int32, (size, size), 1)
        )
        shift_col[low:high, :] = jnp.sum(
            jnp.where(square, shift[:, low:high], 0.0), axis=1, keepdims=True
        )

    for copy in act_copies:
        copy.wait()
    per = max(1, min(n, 256 * n // cin))
    groups = n // per
    deep = cin // groups
    zero = jnp.zeros((1, mid), F32)
    total, squares = zero, zero
    for j in range(groups):
        group = lax.rem(lax.div(me, per) + j, groups)
        for i in range(per):
            if j == 0 and i == 0:
                continue
            member = lax.rem(lax.rem(me, per) + i, per)
            arrived(0, group * per + member, whole(0))
        reduce_w = assemble(recv_r.at[pl.ds(group * per, per)])
        columns = pl.ds(pl.multiple_of(group * deep, 128), deep)

        def reduce_step(b, carry):
            total, squares = carry
            x = act[pl.ds(b * step, step), :, :, columns].reshape(rows, deep)
            y = dot(x, reduce_w)
            if j > 0:
                y = y + rows_f32[b]
            rows_f32[b] = y
            if j < groups - 1:
                return carry
            return (
                total + jnp.sum(y, axis=0, keepdims=True),
                squares + jnp.sum(y * y, axis=0, keepdims=True),
            )

        total, squares = lax.fori_loop(0, blocks, reduce_step, (total, squares))
    stat1[zz, 0:1] = total
    stat1[zz, 1:2] = squares
    copies = share(stat1, 0)
    blend_and_send(3)
    for copy in copies:
        copy.wait()
    scale1, offset1 = scale_of(finish(stat1), mean1_out, var1_out, 0, mid)

    def first_step(b, carry):
        y = jnp.maximum(rows_f32[b] * scale1 + offset1, 0.0)
        wide[pl.ds(b * step + 1, step), 1 : side + 1] = y.astype(BF16).reshape(
            step, side, images, mid
        )
        return carry

    lax.fori_loop(0, blocks, first_step, 0)

    all_arrived(1, whole(1))
    spatial_w = assemble(recv_s)

    def spatial_step(b, carry):
        total, squares = carry
        taps = [
            wide[pl.ds(b * step + dy, step), dx : dx + side].reshape(rows, mid)
            for dy in range(3)
            for dx in range(3)
        ]
        y = dot(jnp.concatenate(taps, axis=1), spatial_w)
        rows_f32[b] = y
        return (
            total + jnp.sum(y, axis=0, keepdims=True),
            squares + jnp.sum(y * y, axis=0, keepdims=True),
        )

    total, squares = lax.fori_loop(0, blocks, spatial_step, (zero, zero))
    stat2[zz, 0:1] = total
    stat2[zz, 1:2] = squares
    copies = share(stat2, 1)
    for copy in copies:
        copy.wait()
    scale2, offset2 = scale_of(finish(stat2), mean2_out, var2_out, mid, 2 * mid)

    passed = []
    if half:
        all_arrived(3, pl.ds(mine_low, half))
        block = recv_c.at[:, pl.ds(mine_low, half), :]
        copy = pltpu.make_async_remote_copy(
            src_ref=block,
            dst_ref=block,
            send_sem=pair.at[0],
            recv_sem=pair.at[1],
            device_id=(me, zz + 1 - 2 * low_bit),
            device_id_type=MESH,
        )
        copy.start()
        passed.append(copy)

    def second_step(b, carry):
        gram, total = carry
        y = jnp.maximum(rows_f32[b] * scale2 + offset2, 0.0)
        y = y.astype(BF16)
        second[b] = y
        return (
            gram + dot(y, y, ((0,), (0,))),
            total + jnp.sum(y.astype(F32), axis=0, keepdims=True),
        )

    gram, total = lax.fori_loop(
        0, blocks, second_step, (jnp.zeros((mid, mid), F32), zero)
    )
    all_arrived(2, whole(2))
    expand_w = assemble(recv_e)

    def exact(a):
        high = a.astype(BF16)
        rest = a - high.astype(F32)
        middle = rest.astype(BF16)
        low = (rest - middle.astype(F32)).astype(BF16)
        return dot(high, expand_w) + (dot(middle, expand_w) + dot(low, expand_w))

    stat3[zz, 0:1] = exact(jnp.broadcast_to(total, (16, mid)))[0:1]
    stat3[zz, 1:2] = jnp.sum(exact(gram) * expand_w.astype(F32), axis=0, keepdims=True)
    copies = share(stat3, 2)
    for copy in copies:
        copy.wait()
    scale3, offset3 = scale_of(
        finish(stat3), mean3_out, var3_out, 2 * mid, 2 * mid + cin
    )

    area = side * images
    pooled_f32[...] = jnp.zeros_like(pooled_f32)

    def expand_step(i, carry):
        at = pl.ds(pl.multiple_of(lax.rem(i, step) * area, 16), area)
        x = second[i // step, at, :]
        wide_step = 256 if cin % 256 == 0 else cin
        for low in range(0, cin, wide_step):
            cut = slice(low, low + wide_step)
            e = dot(x, expand_w[:, cut]) * scale3[:, cut] + offset3[:, cut]
            e = e.reshape(side, images, wide_step) + act[i, :, :, cut].astype(F32)
            pooled_f32[:, cut] += jnp.sum(jnp.maximum(e, 0.0), axis=0)
        return carry

    lax.fori_loop(0, side, expand_step, 0)
    pooled = (pooled_f32[...] / float(side * side)).astype(BF16)
    all_arrived(4, rest_rows)
    for copy in passed:
        copy.wait()

    width = cin // n
    if width % 128 == 0:
        class_w = jnp.concatenate([recv_c[q] for q in range(n)], axis=1)
        logits = dot(class_w, pooled, ((1,), (1,)))
    else:
        logits = jnp.zeros((classes, images), F32)
        for q in range(n):
            part = pooled[:, q * width : (q + 1) * width]
            logits = logits + dot(recv_c[q], part, ((1,), (1,)))
    logits = logits + shift_col[...]
    class_ids = lax.broadcasted_iota(jnp.int32, (classes, images), 0)
    hit = class_ids == labels_ref[...]
    correct = jnp.sum(jnp.where(hit, logits, 0.0), axis=0, keepdims=True)
    rival = jnp.max(jnp.where(hit, -1e30, logits), axis=0, keepdims=True)
    margin = jnp.sum(correct - rival, axis=1, keepdims=True) / float(nb * images)
    mine = me * nb + zz
    margins[mine] = jnp.broadcast_to(margin, margins.shape[1:])
    copies = []
    for i, other in enumerate(others):
        copy = pltpu.make_async_remote_copy(
            src_ref=margins.at[mine],
            dst_ref=margins.at[mine],
            send_sem=msend.at[i],
            recv_sem=mrecv.at[i],
            device_id=other,
            device_id_type=MESH,
        )
        copy.start()
        copies.append(copy)
    for group in sends:
        for copy in group:
            copy.wait_send()
    for copy in copies:
        copy.wait()
    lanes = lax.broadcasted_iota(jnp.int32, (1, 128), 1)
    result = jnp.zeros((1, 128), F32)
    for q in range(n):
        part = margins[q * nb]
        for z in range(1, nb):
            part = part + margins[q * nb + z]
        result = jnp.where(lanes == q, part, result)
    margin_out[...] = result


def hand_over(*refs):
    for source, target in zip(refs[:6], refs[7:13]):
        target[...] = source[...]
    points = refs[13].shape[0]
    refs[13][...] = refs[6][0, 0:points]


def shards(
    n,
    nb,
    activations,
    labels,
    t_values,
    point_index,
    w_reduce,
    w_spatial,
    w_expand,
    w_classes,
    norm_gain,
    norm_bias,
    class_bias,
):
    images, side, _, cin = activations.shape
    mid = w_reduce.shape[2]
    classes = w_classes.shape[1]
    step = block_of(side)
    blocks = side // step
    rows = step * side * images
    cfg = (n, nb, images, side, cin, mid, classes, step)
    smem = pl.BlockSpec(memory_space=pltpu.SMEM)
    vmem = pl.BlockSpec(memory_space=pltpu.VMEM)
    hbm = pl.BlockSpec(memory_space=pltpu.HBM)

    def slices(parts):
        return [
            pltpu.VMEM((parts,) + w_reduce.shape[1:], BF16),
            pltpu.VMEM((parts,) + w_spatial.shape[1:], BF16),
            pltpu.VMEM((parts,) + w_expand.shape[1:], BF16),
            pltpu.VMEM((parts,) + w_classes.shape[1:], BF16),
        ]

    dma = pltpu.SemaphoreType.DMA
    outs = pl.pallas_call(
        functools.partial(kernel, cfg),
        out_shape=[
            jax.ShapeDtypeStruct((1, mid), F32),
            jax.ShapeDtypeStruct((1, mid), F32),
            jax.ShapeDtypeStruct((1, mid), F32),
            jax.ShapeDtypeStruct((1, mid), F32),
            jax.ShapeDtypeStruct((1, cin), F32),
            jax.ShapeDtypeStruct((1, cin), F32),
            jax.ShapeDtypeStruct((1, 128), F32),
        ],
        in_specs=[smem, smem, vmem, vmem, vmem, vmem, hbm, hbm, hbm, hbm, hbm],
        out_specs=[vmem] * 7,
        scratch_shapes=[
            pltpu.VMEM((side, side, images, cin), BF16),
            *slices(3),
            *slices(n - 1),
            *slices(n),
            pltpu.VMEM((blocks, rows, mid), F32),
            pltpu.VMEM((side + 2, side + 2, images, mid), BF16),
            pltpu.VMEM((blocks, rows, mid), BF16),
            pltpu.VMEM((images, cin), F32),
            pltpu.VMEM((classes, 1), F32),
            pltpu.VMEM((nb, 2, mid), F32),
            pltpu.VMEM((nb, 2, mid), F32),
            pltpu.VMEM((nb, 2, cin), F32),
            pltpu.VMEM((n * nb, 1, 128), F32),
            dma((4,)),
            dma((blocks,)),
            dma((5, n)),
            dma((5, n)),
            dma((2,)),
            dma((3, nb - 1)),
            dma((3, nb - 1)),
            dma((n * nb - 1,)),
            dma((n * nb - 1,)),
        ],
        compiler_params=pltpu.CompilerParams(
            collective_id=0, has_side_effects=True, vmem_limit_bytes=62 * 1024 * 1024
        ),
    )(
        t_values,
        point_index,
        labels[None, :],
        norm_gain,
        norm_bias,
        class_bias,
        jnp.transpose(activations, (1, 2, 0, 3)),
        w_reduce,
        w_spatial,
        w_expand,
        w_classes,
    )
    points = point_index.shape[0]
    return pl.pallas_call(
        hand_over,
        out_shape=[jax.ShapeDtypeStruct(o.shape, F32) for o in outs[:6]]
        + [jax.ShapeDtypeStruct((points,), F32)],
        in_specs=[vmem] * 7,
        out_specs=[vmem] * 7,
    )(*outs)


def solution(mesh):
    n, nb = mesh.shape["point"], mesh.shape["batch"]
    placed = (
        P("batch", None, None, None),
        P("batch"),
        P(),
        P(),
        P(None, "point", None),
        P(None, "point", None),
        P(None, "point", None),
        P(None, None, "point"),
        P(),
        P(),
        P(),
    )
    return jax.shard_map(
        functools.partial(shards, n, nb),
        mesh=mesh,
        in_specs=placed,
        out_specs=(
            P("point", None),
            P("point", None),
            P("point", None),
            P("point", None),
            P("point", None),
            P("point", None),
            P(),
        ),
        check_vma=False,
    )
```
